32 devices in a mesh: dp: 32 (over z, y, x, core).
Axes of the slice: x: 2, y: 2, z: 4, core: 2. Of those that a mesh axis runs over, the one named last changes fastest.
Arguments:
- tokens: bfloat16 [24576, 1024], P('dp'), may hold values from -6 to 6
- seg_ids: int32 [96, 256], P('dp'), may hold values from 0 to 7, never falling along the last dimension, each value on 1 to 128 neighbouring positions
- w_qkv: bfloat16 [1024, 3072], P('dp'), may hold values from -0.1875 to 0.1875
- w_attn_out: bfloat16 [1024, 1024], P('dp'), may hold values from -1 to 1
- w_in: bfloat16 [1024, 5248], P('dp'), may hold values from -0.1875 to 0.1875
- w_down: bfloat16 [2624, 1024], P(None, 'dp'), may hold values from -0.125 to 0.125
- gain_attn: bfloat16 [1024], P('dp'), may hold values from 0.099609375 to 1.8984375
- gain_mlp: bfloat16 [1024], P('dp'), may hold values from 0.099609375 to 1.8984375
- cotangent: bfloat16 [24576, 1024], P('dp'), may hold values from -6 to 6
Outputs:
- out: bfloat16 [24576, 1024], P('dp')
- tokens_grad: float32 [24576, 1024], P('dp')
- grad_qkv: float32 [1024, 3072], P('dp')
- grad_attn_out: float32 [1024, 1024], P('dp')
- grad_in: float32 [1024, 5248], P('dp')
- grad_down: float32 [2624, 1024], P(None, 'dp')
- grad_gain_attn: float32 [1024], P('dp')
- grad_gain_mlp: float32 [1024], P('dp')
The draws below stay inside these ranges and needn't reach their ends.
Inputs may be any that keep to these rules, and one draw needn't show every extreme that they name: `seg_ids`: in each micro-batch the numbers never fall along the 256 slots and all 8 numbers occur; each run of equal numbers is one sequence of 1 to 128 tokens, and some run in the draw is exactly 128 long.
All inputs are finite; a program needn't handle non-finite values.
Results may differ from the reference program's by a relative error of at most 0.012.
The reference program's roundings to bfloat16 on the way count: a program that leaves them out, or rounds other values in their place, can miss the bound.
Values may be sent and summed in bfloat16 or wider, within the bound.
No kernel may reach another device: no remote copies, remote signals or barrier semaphores. Data moves between devices by JAX's collectives and lax.ppermute only.
A program may use at most 256 MiB of HBM per device.

```python
import math
import jax
import jax.numpy as jnp
import numpy as np
from jax import lax

D = 1024
FF = 2624
HEADS = 16
HEAD_DIM = 64
SEQS = 8
MB_TOK = 256
BATCHES = 96
TOKENS = 24576


def strengthened(array, stream_key, source, target, parts, factor):
    owner, partner = [(jnp.arange(array.shape[dim]) // (array.shape[dim] // parts)).reshape([-1 if axis == dim else 1 for axis in range(array.ndim)]) for dim in (source, target)]
    chosen = jax.random.permutation(stream_key, parts)[partner]
    strong = (owner == chosen) | (owner == (partner + parts // 2) % parts)
    return jnp.where(strong, factor * array, array)


def steps_of(rng, extent, pieces, least, top_value):
    level = 1.0
    for dim, blocks in pieces:
        steps = jax.random.uniform(jax.random.fold_in(jax.random.fold_in(rng, 6), dim), (blocks,), jnp.float32, least / len(pieces), top_value / len(pieces))
        level = level * jnp.repeat(jnp.exp(steps), extent[dim] // blocks).reshape((-1,) + (1,) * (len(extent) - 1 - dim))
    return level


def split_up(count, total, bound, lean):
    weights = [(1 << 20) // math.isqrt(standing ** lean) + 1 for standing in range(2, count + 1)]
    rest, given = total - bound - (count - 1), [1] * (count - 1)
    while rest > 0:
        movable = [i for i in range(count - 1) if given[i] < bound]
        pool, budget = sum([weights[i] for i in movable]), rest
        for i in movable:
            more = min(bound - given[i], max(1, budget * weights[i] // pool), rest)
            given[i] = given[i] + more
            rest = rest - more
    return np.array([bound] + given)


def uneven_parts(rng, count, total, most, skew):
    if count == 2:
        one = jax.random.randint(rng, (), max(1, total - most), min(most, total - 1) + 1)
        return jnp.stack([one, total - one])
    sizes = jnp.asarray(split_up(count, total, most, skew), jnp.int32)
    twos = (count - 1) // 2
    donor, taker = sizes[1:1 + 2 * twos:2], sizes[2:2 + 2 * twos:2]
    slack = jnp.minimum(donor - 1, most - taker)
    passed = jax.random.randint(jax.random.fold_in(rng, 1), (twos,), 0, 1 << 20) % (slack + 1)
    sizes = sizes.at[1:1 + 2 * twos:2].set(donor - passed).at[2:2 + 2 * twos:2].set(taker + passed)
    return sizes[jax.random.permutation(jax.random.fold_in(rng, 2), count)]


def normal_values(rng, dims, scale, most, pieces=(), kind=jnp.bfloat16):
    level = steps_of(rng, dims, pieces, -0.22, 0.18) if pieces else 1.0
    entries = jax.random.normal(rng, dims, jnp.float32) * scale * level
    return jnp.minimum(jnp.maximum(entries, -most), most).astype(kind)


def bell_draw_with(rng, dims, scale, reach, split, heavy, kind=jnp.bfloat16):
    array = scale * jax.random.normal(rng, dims, jnp.float32)
    if split:
        array = array * steps_of(rng, dims, split, -0.22, 0.18)
    return jnp.clip(strengthened(array, jax.random.fold_in(rng, 3), *heavy), -reach, reach).astype(kind)


def setup_inputs(seed: int = 0) -> dict:
    key_list = jax.random.split(jax.random.key(seed), 10)
    return {
        "tokens": normal_values(key_list[0], (TOKENS, D), 1.0, 6.0, ((0, 32),)),
        "seg_ids": jax.vmap(lambda own: jnp.searchsorted(jnp.cumsum(uneven_parts(own, SEQS, MB_TOK, MB_TOK // 2, 2)), jnp.arange(MB_TOK), side="right"))(jax.random.split(key_list[1], BATCHES)).reshape((BATCHES, MB_TOK)).astype(jnp.int32),
        "w_qkv": normal_values(key_list[2], (D, 3 * D), D ** -0.5, 0.1875, ((0, 32),)),
        "w_attn_out": normal_values(key_list[3], (D, D), (D // 32) ** -0.5, 1.0, ((0, 32),)),
        "w_in": normal_values(key_list[4], (D, 2 * FF), D ** -0.5, 0.1875, ((0, 32),)),
        "w_down": normal_values(key_list[5], (FF, D), FF ** -0.5, 0.125, ((1, 32),)),
        "gain_attn": jnp.clip(1.0 + 0.18 * jax.random.normal(key_list[6], (D,), jnp.float32), 0.099609375, 1.8984375).astype(jnp.bfloat16),
        "gain_mlp": jnp.clip(1.0 + 0.18 * jax.random.normal(key_list[7], (D,), jnp.float32), 0.099609375, 1.8984375).astype(jnp.bfloat16),
        "cotangent": bell_draw_with(key_list[8], (TOKENS, D), 1.0, 6.0, ((0, 32),), (0, 1, 32, 2.75)),
    }


EPSILON = 1e-05
THETA = 160000.0
NEG_BIG = -1e+30
ROOT_HALF = 0.7071067811865476

@jax.custom_vjp
def low(v):
    return lax.optimization_barrier(v.astype(jnp.bfloat16)).astype(jnp.float32)

@jax.custom_vjp
def low_back(v):
    return v

def low_keep(v):
    return (low(v), None)

def low_pass(kept, grad):
    return (grad,)

def back_keep(v):
    return (v, None)

def back_low(kept, grad):
    return (low(grad),)
low.defvjp(low_keep, low_pass)
low_back.defvjp(back_keep, back_low)

def positions(seg_row):
    column = lax.broadcasted_iota(jnp.int32, seg_row.shape, seg_row.ndim - 1)
    before = jnp.concatenate([jnp.full(seg_row.shape[:-1] + (1,), -1, jnp.int32), seg_row[..., :-1].astype(jnp.int32)], axis=-1)
    starts = lax.cummax(jnp.where(seg_row.astype(jnp.int32) != before, column, 0).astype(jnp.int32), axis=seg_row.ndim - 1)
    return (column - starts).astype(jnp.int32)

def rotary_tables(offsets):
    halves = HEAD_DIM // 2
    frequency = jnp.power(jnp.float32(THETA), -(jnp.arange(halves, dtype=jnp.float32) * 2.0 / HEAD_DIM))
    angles = offsets.astype(jnp.float32)[:, None] * frequency[None, :]
    angles = jnp.concatenate([angles, angles], axis=-1)
    return (jnp.cos(angles)[:, None, :], jnp.sin(angles)[:, None, :])

def rotate(field):
    halves = field.shape[-1] // 2
    return jnp.concatenate([-field[..., halves:], field[..., :halves]], axis=-1)

def gelu_exact(field):
    return 0.5 * field * (1.0 + lax.erf(field * ROOT_HALF))

def layer_norm(field, gain_row):
    center = field - lax.optimization_barrier(jnp.mean(field, axis=-1, keepdims=True))
    return center * lax.rsqrt(lax.optimization_barrier(jnp.mean(center * center, axis=-1, keepdims=True)) + EPSILON) * gain_row

def matmul(factor_left, factor_right):
    return jnp.dot(factor_left, factor_right, precision=lax.Precision.HIGHEST)

def forward(inputs, seg_row, w_qkv, w_attn_out, w_in, w_down, gain_attn, gain_mlp):
    block_rows = inputs.shape[0]
    cosine_table, sine_table = rotary_tables(positions(seg_row))
    normed = low(layer_norm(inputs, gain_attn))
    projected = low_back(matmul(normed, w_qkv))
    queries = projected[:, :D].reshape(block_rows, HEADS, HEAD_DIM)
    keys_rot = projected[:, D:2 * D].reshape(block_rows, HEADS, HEAD_DIM)
    values = low(projected[:, 2 * D:].reshape(block_rows, HEADS, HEAD_DIM))
    queries = low(queries * cosine_table + rotate(queries) * sine_table)
    keys_rot = low(keys_rot * cosine_table + rotate(keys_rot) * sine_table)
    scores = low_back(jnp.einsum('qhd,khd->hqk', queries, keys_rot, precision=lax.Precision.HIGHEST) * HEAD_DIM ** (-0.5))
    same_seq = seg_row[:, None] == seg_row[None, :]
    scores = jnp.where(same_seq[None], scores, NEG_BIG)
    exponent = jnp.exp(scores - lax.optimization_barrier(jnp.max(scores, axis=-1, keepdims=True)))
    probability = low(exponent / lax.optimization_barrier(jnp.sum(exponent, axis=-1, keepdims=True)))
    attended = jnp.einsum('hqk,khd->qhd', probability, values, precision=lax.Precision.HIGHEST)
    attended = low(low_back(attended)).reshape(block_rows, D)
    resid = inputs + low_back(matmul(attended, w_attn_out))
    normed_mlp = low(layer_norm(resid, gain_mlp))
    gate_up = low_back(matmul(normed_mlp, w_in))
    hidden = low(gelu_exact(gate_up[:, :FF]) * gate_up[:, FF:])
    return resid + low_back(matmul(hidden, w_down))

def reference(tokens, seg_ids, w_qkv, w_attn_out, w_in, w_down, gain_attn, gain_mlp, cotangent):
    batch_count, block_rows = seg_ids.shape
    weights = tuple((param.astype(jnp.float32) for param in (w_qkv, w_attn_out, w_in, w_down, gain_attn, gain_mlp)))
    inputs = tokens.astype(jnp.float32).reshape(batch_count, block_rows, D)
    grads_given = cotangent.astype(jnp.float32).reshape(batch_count, block_rows, D)
    zeros_init = tuple((jnp.zeros(param.shape, jnp.float32) for param in weights))

    def scan_step(totals, stacked):
        block_in, seg_row, block_cot = stacked

        def local_fn(field, *params):
            return forward(field, seg_row, *params)
        result, pull = jax.vjp(local_fn, block_in, *weights)
        pulled = pull(block_cot)
        totals = tuple((summed + extra for summed, extra in zip(totals, pulled[1:])))
        return (totals, (result.astype(jnp.bfloat16), pulled[0]))
    totals, (results, input_grads) = lax.scan(scan_step, zeros_init, (inputs, seg_ids, grads_given))
    return (results.reshape(batch_count * block_rows, D), input_grads.reshape(batch_count * block_rows, D), totals[0], totals[1], totals[2], totals[3], totals[4], totals[5])
```

```python
import functools

import jax
import jax.numpy as jnp
from jax import lax
from jax.experimental import pallas as pl
from jax.experimental.pallas import tpu as pltpu
from jax.sharding import PartitionSpec as P

HEADS = 16
HEAD_DIM = 64
EPSILON = 1e-05
THETA = 160000.0
NEG_BIG = -1e30
ROOT_HALF = 0.7071067811865476
INV_ROOT_TWO_PI = 0.3989422804014327
SCALE = HEAD_DIM ** (-0.5)
LANES = 128
PARTS = 4
F32 = jnp.float32
BF16 = jnp.bfloat16


def up_to(count, unit):
    return -(-count // unit) * unit


def mm(left, right, dims=((1,), (0,))):
    return lax.dot_general(left, right, (dims, ((), ())), preferred_element_type=F32)


def exchange(value, bit_of):
    count = lax.axis_size("dp")
    return lax.ppermute(value, "dp", [(i, i ^ (1 << bit_of(i))) for i in range(count)])


def bit_orders(count):
    top = count.bit_length() - 1
    even = list(range(top))
    odd = list(range(top))
    if top >= 3:
        odd[1], odd[2] = odd[2], odd[1]
    return even, odd


def gather_rows(shard, beside=()):
    count = lax.axis_size("dp")
    even, odd = bit_orders(count)
    index = lax.axis_index("dp")
    is_odd = index & 1
    rows, width = shard.shape
    top = len(even)
    held = shard[None]
    for step in reversed(range(top)):
        arrived = exchange(held, lambda i: even[step] if i & 1 == 0 else odd[step])
        mine = jnp.where(is_odd == 0, (index >> even[step]) & 1, (index >> odd[step]) & 1)
        both = jnp.zeros((held.shape[0], 2, rows, width), held.dtype)
        both = lax.dynamic_update_slice(both, held[:, None], (0, mine, 0, 0))
        if step < min(2, top - 1):
            arrived, both, beside = lax.optimization_barrier((arrived, both, beside))
        both = lax.dynamic_update_slice(both, arrived[:, None], (0, 1 - mine, 0, 0))
        if step == 1 and top >= 3:
            quad = both.reshape(-1, 2, 2, rows, width)
            both = jnp.where(is_odd == 0, quad, quad.swapaxes(1, 2))
        held = both.reshape(-1, rows, width)
    return held.reshape(count * rows, width), beside


def chip_steps(count):
    even = list(range(count.bit_length() - 2))
    return even, [1, 0] + even[2:]


def sum_order(core, width):
    even, odd = chip_steps(lax.axis_size("dp"))
    chip = lax.axis_index("dp") >> 1
    rows = width >> len(even)
    column = lax.broadcasted_iota(jnp.int32, (1, width), 1)
    owner = jnp.zeros_like(column) + chip
    for step in range(len(even)):
        given = 1 - ((column >> (width.bit_length() - 2 - step)) & 1)
        owner = owner ^ (given << jnp.where(core == 0, even[step], odd[step]))
    source = owner * rows + column % rows
    return (lax.broadcasted_iota(jnp.int32, (width, width), 0) == source).astype(BF16)


def to_partner(value):
    return exchange(value, lambda i: 0)


class Reduction:
    def __init__(self, given, held):
        self.even, self.odd = chip_steps(lax.axis_size("dp"))
        self.step = 0
        self.given, self.held, self.arrived = given, held, None

    def prepare(self):
        if self.step:
            half = self.held.shape[0] // 2
            held, arrived = self.held, self.arrived
            self.given = (held[:half] + arrived[:half].astype(F32)).astype(BF16)
            self.held = held[half:] + arrived[half:].astype(F32)
        return self.given

    def send(self, given):
        even, odd = self.even[self.step] + 1, self.odd[self.step] + 1
        self.arrived = exchange(given, lambda i: even if i & 1 == 0 else odd)
        self.step += 1

    def done(self):
        return self.step == len(self.even)

    def result(self):
        return self.held.astype(F32) + self.arrived.astype(F32)


class Send:
    def __init__(self, value):
        self.value, self.arrived = value, None

    def prepare(self):
        return self.value

    def send(self, value):
        self.arrived = to_partner(value)

    def done(self):
        return self.arrived is not None


class Clock:
    def __init__(self):
        self.last = ()

    def stage(self, inputs, reductions=()):
        reductions = [r for r in reductions if not r.done()]
        sent = [r.prepare() for r in reductions]
        inputs, sent, _ = lax.optimization_barrier((inputs, sent, self.last))
        for reduction, other in zip(reductions, sent):
            reduction.send(other)
        return inputs

    def end(self, *results):
        self.last = results


def turned(field):
    lane = lax.broadcasted_iota(jnp.int32, field.shape, 1)
    return jnp.where(
        lane % HEAD_DIM < HEAD_DIM // 2,
        pltpu.roll(field, LANES - HEAD_DIM // 2, 1),
        pltpu.roll(field, HEAD_DIM // 2, 1),
    )


def forward_kernel(p_ref, cos_ref, sin_ref, col_ref, row_ref, qkv_ref, a_ref):
    cosine, sine = cos_ref[...], sin_ref[...]
    same = col_ref[0] == row_ref[0]
    width = a_ref.shape[1]
    lane = lax.broadcasted_iota(jnp.int32, cosine.shape, 1)
    first = lane < HEAD_DIM
    for part in range(width // LANES):
        q_at, k_at, v_at = (pl.ds(which * width + part * LANES, LANES) for which in range(3))
        q, k = p_ref[:, q_at], p_ref[:, k_at]
        q = (q * cosine + turned(q) * sine).astype(BF16)
        k = (k * cosine + turned(k) * sine).astype(BF16)
        v = p_ref[:, v_at].astype(BF16)
        qkv_ref[:, q_at], qkv_ref[:, k_at], qkv_ref[:, v_at] = q, k, v
        scaled = q.astype(F32) * SCALE
        results = []
        for head in range(2):
            own = first if head == 0 else jnp.logical_not(first)
            q_own = jnp.where(own, scaled, 0.0).astype(BF16)
            scores = jnp.where(same, mm(q_own, k, ((1,), (1,))), NEG_BIG)
            exponent = jnp.exp(scores - jnp.max(scores, axis=1, keepdims=True))
            chance = exponent * (1.0 / jnp.sum(exponent, axis=1, keepdims=True))
            results.append(mm(chance.astype(BF16), v))
        a_ref[:, pl.ds(part * LANES, LANES)] = jnp.where(first, results[0], results[1]).astype(BF16)


def backward_kernel(qkv_ref, ga_ref, cos_ref, sin_ref, col_ref, row_ref, g_ref):
    cosine, sine = cos_ref[...], sin_ref[...]
    same = col_ref[0] == row_ref[0]
    width = ga_ref.shape[1]
    lane = lax.broadcasted_iota(jnp.int32, cosine.shape, 1)
    first = lane < HEAD_DIM
    for part in range(width // LANES):
        q_at, k_at, v_at = (pl.ds(which * width + part * LANES, LANES) for which in range(3))
        q, k, v = qkv_ref[:, q_at], qkv_ref[:, k_at], qkv_ref[:, v_at]
        ga = ga_ref[:, pl.ds(part * LANES, LANES)]
        scaled = q.astype(F32) * SCALE
        q_low = scaled.astype(BF16)
        ga_wide = ga.astype(F32)
        gqs, gks, gvs = [], [], []
        for head in range(2):
            own = first if head == 0 else jnp.logical_not(first)
            q_own = jnp.where(own, scaled, 0.0).astype(BF16)
            ga_own = jnp.where(own, ga_wide, 0.0).astype(BF16)
            scores = jnp.where(same, mm(k, q_own, ((1,), (1,))), NEG_BIG)
            exponent = jnp.exp(scores - jnp.max(scores, axis=0, keepdims=True))
            chance = exponent * (1.0 / jnp.sum(exponent, axis=0, keepdims=True))
            gvs.append(mm(chance.astype(BF16), ga))
            g_chance = mm(v, ga_own, ((1,), (1,)))
            inner = jnp.sum(g_chance * chance, axis=0, keepdims=True)
            g_scores = (chance * (g_chance - inner)).astype(BF16)
            gks.append(mm(g_scores, q_low))
            gqs.append(mm(g_scores, k, ((0,), (0,))))
        gq = jnp.where(first, gqs[0], gqs[1]) * SCALE
        gk = jnp.where(first, gks[0], gks[1])
        g_ref[:, q_at] = (gq * cosine + turned(gq * sine)).astype(BF16)
        g_ref[:, k_at] = (gk * cosine + turned(gk * sine)).astype(BF16)
        g_ref[:, v_at] = jnp.where(first, gvs[0], gvs[1]).astype(BF16)


def attention_specs(block):
    table = pl.BlockSpec((block, LANES), lambda b, h, *_: (b, 0))
    column = pl.BlockSpec((1, block, 1), lambda b, h, *_: (b, 0, 0))
    row = pl.BlockSpec((1, 1, block), lambda b, h, *_: (b, 0, 0))
    return [table, table, column, row]


def attention_forward(projected, cosine, sine, seg_ids):
    blocks, block = seg_ids.shape
    total = projected.shape[1]
    whole = pl.BlockSpec((block, total // PARTS), lambda b, h: (b, h))
    third = pl.BlockSpec((block, total // PARTS // 3), lambda b, h: (b, h))
    rows = projected.shape[0]
    return pl.pallas_call(
        forward_kernel,
        grid=(blocks, PARTS),
        in_specs=[whole] + attention_specs(block),
        out_specs=[whole, third],
        out_shape=[
            jax.ShapeDtypeStruct((rows, total), BF16),
            jax.ShapeDtypeStruct((rows, total // 3), BF16),
        ],
        name="attention_forward",
    )(projected, cosine, sine, seg_ids[:, :, None], seg_ids[:, None, :])


def attention_backward(qkv, grad_att, cosine, sine, seg_ids, start, parts):
    blocks, block = seg_ids.shape
    wide, narrow = qkv.shape[1] // PARTS, grad_att.shape[1] // PARTS

    def kernel(start_ref, *refs):
        backward_kernel(*refs)

    return pl.pallas_call(
        kernel,
        grid_spec=pltpu.PrefetchScalarGridSpec(
            num_scalar_prefetch=1,
            grid=(blocks, parts),
            in_specs=[
                pl.BlockSpec((block, wide), lambda b, h, start_ref: (b, start_ref[0] + h)),
                pl.BlockSpec((block, narrow), lambda b, h, start_ref: (b, start_ref[0] + h)),
            ]
            + attention_specs(block),
            out_specs=pl.BlockSpec((block, wide), lambda b, h, start_ref: (b, h)),
        ),
        out_shape=jax.ShapeDtypeStruct((qkv.shape[0], wide * parts), BF16),
        name="attention_backward",
    )(start[None], qkv, grad_att, cosine, sine, seg_ids[:, :, None], seg_ids[:, None, :])


def tables(seg_ids):
    column = lax.broadcasted_iota(jnp.int32, seg_ids.shape, 1)
    before = jnp.concatenate([jnp.full_like(seg_ids[:, :1], -1), seg_ids[:, :-1]], axis=1)
    starts = lax.cummax(jnp.where(seg_ids != before, column, 0), axis=1)
    offsets = (column - starts).reshape(-1)
    halves = HEAD_DIM // 2
    frequency = jnp.power(F32(THETA), -(jnp.arange(halves, dtype=F32) * 2.0 / HEAD_DIM))
    angles = offsets.astype(F32)[:, None] * frequency[None, :]
    cosine, sine = jnp.cos(angles), jnp.sin(angles)
    return (
        jnp.concatenate([cosine] * 4, axis=1),
        jnp.concatenate([-sine, sine, -sine, sine], axis=1),
    )


def gelu_exact(field):
    return 0.5 * field * (1.0 + lax.erf(field * ROOT_HALF))


def gelu_slope(field):
    return (
        0.5 * (1.0 + lax.erf(field * ROOT_HALF))
        + field * jnp.exp(-0.5 * field * field) * INV_ROOT_TWO_PI
    )


def norm_unit(field):
    center = field - jnp.mean(field, axis=-1, keepdims=True)
    inv_scale = lax.rsqrt(jnp.mean(center * center, axis=-1, keepdims=True) + EPSILON)
    return center * inv_scale, inv_scale


def norm_backward(gradient, unit_rows, inv_scale, gain_row):
    scaled = gradient * gain_row
    inner = (
        scaled
        - jnp.mean(scaled, axis=-1, keepdims=True)
        - unit_rows * jnp.mean(scaled * unit_rows, axis=-1, keepdims=True)
    )
    return inv_scale * inner


def shards(tokens, seg_ids, w_qkv, w_attn_out, w_in, w_down, gain_attn, gain_mlp, cotangent):
    model_width = tokens.shape[1]
    hidden_units = w_down.shape[0]
    padded = up_to(hidden_units, LANES)
    extra = ((0, 0), (0, padded - hidden_units))

    def by_part(field):
        parts = field.reshape(field.shape[0], 3, PARTS, -1)
        return parts.swapaxes(1, 2).reshape(field.shape)

    gains = jnp.pad(jnp.stack([gain_attn, gain_mlp], axis=1), ((0, 0), (0, LANES - 2)))
    rest = lax.all_gather(
        jnp.concatenate(
            [
                w_attn_out,
                jnp.pad(w_in[:, :hidden_units], extra),
                jnp.pad(w_in[:, hidden_units:], extra),
                jnp.pad(w_down.T, extra),
            ],
            axis=1,
        ),
        "dp",
        axis=0,
        tiled=True,
    )
    inputs = tokens.astype(F32)
    first, (cosine, sine, unit_attn, inv_attn) = gather_rows(
        jnp.concatenate([by_part(w_qkv), gains], axis=1), tables(seg_ids) + norm_unit(inputs)
    )
    core = (lax.axis_index("dp") & 1).astype(jnp.int32)
    other = 1 - core
    own_order, other_order = sum_order(core, model_width), sum_order(other, model_width)

    def ordered(field):
        return mm(field, own_order).astype(BF16), mm(field, other_order).astype(BF16)

    dy_own, dy_other = ordered(cotangent)
    wq = first[:, : 3 * model_width]
    gain_rows = first[:, 3 * model_width :].astype(F32).T
    ga, gm = gain_rows[0:1], gain_rows[1:2]

    normed_attn = (unit_attn * ga).astype(BF16)
    projected = mm(normed_attn, wq)
    attn_own, attn_other = ordered(normed_attn)
    qkv, attended = attention_forward(projected, cosine, sine, seg_ids)
    att_own, att_other = ordered(attended)
    rest, att_own, att_other, attn_own, attn_other, dy_own, dy_other = lax.optimization_barrier(
        (rest, att_own, att_other, attn_own, attn_other, dy_own, dy_other)
    )
    wo = rest[:, :model_width]
    wg = rest[:, model_width : model_width + padded]
    wu = rest[:, model_width + padded : model_width + 2 * padded]
    wd = rest[:, model_width + 2 * padded :]
    resid = inputs + mm(attended, wo)
    unit_mlp, inv_mlp = norm_unit(resid)
    normed_mlp = (unit_mlp * gm).astype(BF16)
    mlp_own, mlp_other, normed_mlp = lax.optimization_barrier(ordered(normed_mlp) + (normed_mlp,))
    gate = mm(normed_mlp, wg)
    upward = mm(normed_mlp, wu)
    activated = gelu_exact(gate)
    hidden = (activated * upward).astype(BF16)

    grad_out = cotangent.astype(F32)
    clock = Clock()
    turn = ((0,), (0,))

    def columns(field, start, width):
        return lax.dynamic_slice_in_dim(field, start, width, 1)

    def weight_gradient(rows, cols):
        return mm(rows, cols, turn).astype(BF16)

    def reduction(rows, cols, came):
        half = rows.shape[1] // 2
        given = mm(rows[:, :half], cols, turn) + came[:half].astype(F32)
        held = mm(rows[:, half:], cols, turn) + came[half:].astype(F32)
        return Reduction(given.astype(BF16), held)

    half_down = up_to(padded // 2, LANES)
    shift = padded - half_down
    down_send = Send(weight_gradient(dy_other, columns(hidden, other * shift, half_down)))
    clock.end(down_send.value)

    (dy,) = clock.stage((cotangent,), [down_send])
    grad_hidden = mm(dy, wd)
    grad_gate = (grad_hidden * upward * gelu_slope(gate)).astype(BF16)
    grad_up = (grad_hidden * activated).astype(BF16)
    grad_own = jnp.where(core == 0, grad_gate, grad_up)
    grad_other = jnp.where(core == 0, grad_up, grad_gate)
    clock.end(grad_own, grad_other)

    (rhs,) = clock.stage((grad_other,))
    in_send = Send(weight_gradient(mlp_other, rhs))
    clock.end(in_send.value)

    (rhs,) = clock.stage((columns(hidden, core * shift, half_down),), [in_send])
    down_sum = reduction(dy_own, rhs, down_send.arrived)
    clock.end(down_sum.held)

    lhs, rhs = clock.stage((grad_gate, grad_up), [down_sum])
    grad_normed_mlp = mm(lhs, wg, ((1,), (1,))) + mm(rhs, wu, ((1,), (1,)))
    clock.end(grad_normed_mlp)

    (rhs,) = clock.stage((grad_own,))
    in_sum = reduction(mlp_own, rhs, in_send.arrived)
    clock.end(in_sum.held)

    (grad_normed_mlp,) = clock.stage((grad_normed_mlp,), [down_sum, in_sum])
    grad_resid = grad_out + norm_backward(grad_normed_mlp, unit_mlp, inv_mlp, gm)
    grad_resid_b = grad_resid.astype(BF16)
    half_out = model_width // 2
    out_send = Send(weight_gradient(att_other, columns(grad_resid_b, other * half_out, half_out)))
    clock.end(out_send.value)

    (lhs,) = clock.stage((grad_resid_b,), [out_send])
    grad_att = mm(lhs, wo, ((1,), (1,))).astype(BF16)
    clock.end(grad_att)

    def heads(grad, part, parts):
        return attention_backward(qkv, grad, cosine, sine, seg_ids, part, parts)

    (grad,) = clock.stage((grad_att,), [down_sum])
    g_other = heads(grad, 2 * other, 2)
    qkv_send = Send(weight_gradient(attn_other, g_other))
    clock.end(qkv_send.value)

    (grad,) = clock.stage((grad_att,), [qkv_send, down_sum])
    g_first = heads(grad, 2 * core, 1)
    clock.end(g_first)

    (rhs,) = clock.stage((g_first,), [in_sum])
    out_sum = reduction(att_own, columns(grad_resid_b, core * half_out, half_out), out_send.arrived)
    half = 3 * model_width // 2
    quarter = half // 2
    q0_sum = reduction(attn_own, rhs, qkv_send.arrived[:, :quarter])
    clock.end(q0_sum.held, out_sum.held)

    (grad,) = clock.stage((grad_att,), [q0_sum, out_sum])
    g_second = heads(grad, 2 * core + 1, 1)
    clock.end(g_second)

    (rhs,) = clock.stage((g_second,), [in_sum])
    q1_sum = reduction(attn_own, rhs, qkv_send.arrived[:, quarter:])
    clock.end(q1_sum.held)

    lhs, g_first, g_second = clock.stage((g_other, g_first, g_second), [q1_sum, q0_sum, out_sum])
    grads = jnp.zeros((lhs.shape[0], 2 * half), BF16)
    grads = lax.dynamic_update_slice(grads, lhs, (0, other * half))
    grads = lax.dynamic_update_slice(grads, g_first, (0, core * half))
    grads = lax.dynamic_update_slice(grads, g_second, (0, core * half + quarter))
    grad_normed_attn = mm(grads, wq, ((1,), (1,)))
    clock.end(grad_normed_attn)

    (grad_normed_attn,) = clock.stage((grad_normed_attn,), [q0_sum, q1_sum, out_sum, in_sum])
    tokens_grad = grad_resid + norm_backward(grad_normed_attn, unit_attn, inv_attn, ga)
    clock.end(tokens_grad)

    (lhs,) = clock.stage((hidden,), [q0_sum, q1_sum, out_sum])
    out = (resid + mm(lhs, wd, ((1,), (1,)))).astype(BF16)
    clock.end(out)
    reductions = [q1_sum, q0_sum, out_sum, down_sum, in_sum]
    while not all(r.done() for r in reductions):
        clock.stage((), reductions)
        clock.end()

    def both_halves(*totals):
        total = jnp.concatenate(totals, axis=1)
        rows = total.shape[0] // 2
        mine = lax.dynamic_slice_in_dim(total, core * rows, rows, 0)
        came = to_partner(lax.dynamic_slice_in_dim(total, other * rows, rows, 0))
        low = jnp.where(core == 0, mine, came)
        high = jnp.where(core == 0, came, mine)
        cuts = [sum(t.shape[1] for t in totals[: i + 1]) for i in range(len(totals) - 1)]
        return zip(jnp.split(low, cuts, axis=1), jnp.split(high, cuts, axis=1))

    (down_low, down_high), (gate_rows, up_rows) = both_halves(down_sum.result(), in_sum.result())
    (out_low, out_high), (first_low, first_high), (last_low, last_high) = both_halves(
        out_sum.result(), q0_sum.result(), q1_sum.result()
    )
    grad_wo = jnp.concatenate([out_low, out_high], axis=1)
    quarters = [first_low, last_low, first_high, last_high]
    size = model_width // PARTS
    grad_qkv = jnp.concatenate(
        [q[:, which * size : (which + 1) * size] for which in range(3) for q in quarters], axis=1
    )
    grad_down = jnp.concatenate([down_low[:, :shift], down_high], axis=1)
    grad_in = jnp.concatenate([gate_rows[:, :hidden_units], up_rows[:, :hidden_units]], axis=1)

    def gain_gradient(weight, gradient, gain):
        return jnp.sum(weight.astype(F32) * gradient, axis=1) / gain.astype(F32)

    return (
        out,
        tokens_grad,
        grad_qkv,
        grad_wo,
        grad_in,
        grad_down[:, :hidden_units].T,
        gain_gradient(w_qkv, grad_qkv, gain_attn),
        gain_gradient(w_in, grad_in, gain_mlp),
    )


def solution(mesh):
    rows = P("dp", None)
    return jax.shard_map(
        shards,
        mesh=mesh,
        in_specs=(rows, rows, rows, rows, rows, P(None, "dp"), P("dp"), P("dp"), rows),
        out_specs=(rows, rows, rows, rows, rows, P(None, "dp"), P("dp"), P("dp")),
        check_vma=False,
    )
```

```python
import functools

import jax
import jax.numpy as jnp
from jax import lax
from jax.experimental import pallas as pl
from jax.experimental.pallas import tpu as pltpu
from jax.sharding import PartitionSpec as P

HEADS = 16
HEAD_DIM = 64
EPSILON = 1e-05
THETA = 160000.0
NEG_BIG = -1e30
ROOT_HALF = 0.7071067811865476
INV_ROOT_TWO_PI = 0.3989422804014327
SCALE = HEAD_DIM ** (-0.5)
LANES = 128
PARTS = 4
F32 = jnp.float32
BF16 = jnp.bfloat16


def up_to(count, unit):
    return -(-count // unit) * unit


def mm(left, right, dims=((1,), (0,))):
    return lax.dot_general(left, right, (dims, ((), ())), preferred_element_type=F32)


def exchange(value, bit_of):
    count = lax.axis_size("dp")
    return lax.ppermute(value, "dp", [(i, i ^ (1 << bit_of(i))) for i in range(count)])


def bit_orders(count):
    top = count.bit_length() - 1
    even = list(range(top))
    odd = list(range(top))
    if top >= 3:
        odd[1], odd[2] = odd[2], odd[1]
    return even, odd


def gather_rows(shard, beside=()):
    count = lax.axis_size("dp")
    even, odd = bit_orders(count)
    index = lax.axis_index("dp")
    is_odd = index & 1
    rows, width = shard.shape
    top = len(even)
    held = shard[None]
    for step in reversed(range(top)):
        arrived = exchange(held, lambda i: even[step] if i & 1 == 0 else odd[step])
        mine = jnp.where(is_odd == 0, (index >> even[step]) & 1, (index >> odd[step]) & 1)
        both = jnp.zeros((held.shape[0], 2, rows, width), held.dtype)
        both = lax.dynamic_update_slice(both, held[:, None], (0, mine, 0, 0))
        if step < min(2, top - 1):
            arrived, both, beside = lax.optimization_barrier((arrived, both, beside))
        both = lax.dynamic_update_slice(both, arrived[:, None], (0, 1 - mine, 0, 0))
        if step == 1 and top >= 3:
            quad = both.reshape(-1, 2, 2, rows, width)
            both = jnp.where(is_odd == 0, quad, quad.swapaxes(1, 2))
        held = both.reshape(-1, rows, width)
    return held.reshape(count * rows, width), beside


def chip_steps(count):
    even = list(range(count.bit_length() - 2))
    return even, [1, 0] + even[2:]


def sum_order(core, width):
    even, odd = chip_steps(lax.axis_size("dp"))
    chip = lax.axis_index("dp") >> 1
    rows = width >> len(even)
    column = lax.broadcasted_iota(jnp.int32, (1, width), 1)
    owner = jnp.zeros_like(column) + chip
    for step in range(len(even)):
        given = 1 - ((column >> (width.bit_length() - 2 - step)) & 1)
        owner = owner ^ (given << jnp.where(core == 0, even[step], odd[step]))
    source = owner * rows + column % rows
    return (lax.broadcasted_iota(jnp.int32, (width, width), 0) == source).astype(BF16)


def to_partner(value):
    return exchange(value, lambda i: 0)


class Reduction:
    def __init__(self, given, held):
        self.even, self.odd = chip_steps(lax.axis_size("dp"))
        self.step = 0
        self.given, self.held, self.arrived = given, held, None

    def prepare(self):
        if self.step:
            half = self.held.shape[0] // 2
            held, arrived = self.held, self.arrived
            self.given = (held[:half] + arrived[:half].astype(F32)).astype(BF16)
            self.held = held[half:] + arrived[half:].astype(F32)
        return self.given

    def send(self, given):
        even, odd = self.even[self.step] + 1, self.odd[self.step] + 1
        self.arrived = exchange(given, lambda i: even if i & 1 == 0 else odd)
        self.step += 1

    def done(self):
        return self.step == len(self.even)

    def beside(self, reduction):
        return Reduction(
            jnp.concatenate([self.given, reduction.given], axis=1),
            jnp.concatenate([self.held, reduction.held], axis=1),
        )

    def result(self):
        return self.held.astype(F32) + self.arrived.astype(F32)


class Send:
    def __init__(self, value):
        self.value, self.arrived = value, None

    def prepare(self):
        return self.value

    def send(self, value):
        self.arrived = to_partner(value)

    def done(self):
        return self.arrived is not None

    def landed(self):
        return Landed(self)


class Landed:
    def __init__(self, owner):
        self.owner = owner

    def done(self):
        return False

    def prepare(self):
        return self.owner.arrived

    def send(self, value):
        self.owner.arrived = value


class Clock:
    def __init__(self):
        self.last = ()

    def stage(self, inputs, reductions=()):
        reductions = [r for r in reductions if not r.done()]
        if self.last:
            for reduction in (r for r in reductions if isinstance(r, Reduction) and r.step):
                reduction.arrived, _ = lax.optimization_barrier((reduction.arrived, self.last))
        sent = [r.prepare() for r in reductions]
        inputs, sent, _ = lax.optimization_barrier((inputs, sent, self.last))
        for reduction, other in zip(reductions, sent):
            reduction.send(other)
        return inputs

    def end(self, *results):
        self.last = results


def turned(field):
    lane = lax.broadcasted_iota(jnp.int32, field.shape, 1)
    return jnp.where(
        lane % HEAD_DIM < HEAD_DIM // 2,
        pltpu.roll(field, LANES - HEAD_DIM // 2, 1),
        pltpu.roll(field, HEAD_DIM // 2, 1),
    )


def forward_kernel(n_ref, w_ref, cos_ref, sin_ref, col_ref, row_ref, qkv_ref, a_ref, p_ref):
    p_ref[...] = mm(n_ref[...], w_ref[...])
    cosine, sine = cos_ref[...], sin_ref[...]
    same = col_ref[0] == row_ref[0]
    width = a_ref.shape[1]
    lane = lax.broadcasted_iota(jnp.int32, cosine.shape, 1)
    first = lane < HEAD_DIM
    for part in range(width // LANES):
        q_at, k_at, v_at = (pl.ds(which * width + part * LANES, LANES) for which in range(3))
        q, k = p_ref[:, q_at], p_ref[:, k_at]
        q = (q * cosine + turned(q) * sine).astype(BF16)
        k = (k * cosine + turned(k) * sine).astype(BF16)
        v = p_ref[:, v_at].astype(BF16)
        qkv_ref[:, q_at], qkv_ref[:, k_at], qkv_ref[:, v_at] = q, k, v
        scaled = q.astype(F32) * SCALE
        results = []
        for head in range(2):
            own = first if head == 0 else jnp.logical_not(first)
            q_own = jnp.where(own, scaled, 0.0).astype(BF16)
            scores = jnp.where(same, mm(q_own, k, ((1,), (1,))), NEG_BIG)
            exponent = jnp.exp(scores - jnp.max(scores, axis=1, keepdims=True))
            chance = exponent * (1.0 / jnp.sum(exponent, axis=1, keepdims=True))
            results.append(mm(chance.astype(BF16), v))
        a_ref[:, pl.ds(part * LANES, LANES)] = jnp.where(first, results[0], results[1]).astype(BF16)


def backward_kernel(qkv_ref, ga_ref, cos_ref, sin_ref, col_ref, row_ref, g_ref):
    cosine, sine = cos_ref[...], sin_ref[...]
    same = col_ref[0] == row_ref[0]
    width = ga_ref.shape[1]
    lane = lax.broadcasted_iota(jnp.int32, cosine.shape, 1)
    first = lane < HEAD_DIM
    for part in range(width // LANES):
        q_at, k_at, v_at = (pl.ds(which * width + part * LANES, LANES) for which in range(3))
        q, k, v = qkv_ref[:, q_at], qkv_ref[:, k_at], qkv_ref[:, v_at]
        ga = ga_ref[:, pl.ds(part * LANES, LANES)]
        scaled = q.astype(F32) * SCALE
        q_low = scaled.astype(BF16)
        ga_wide = ga.astype(F32)
        gqs, gks, gvs = [], [], []
        for head in range(2):
            own = first if head == 0 else jnp.logical_not(first)
            q_own = jnp.where(own, scaled, 0.0).astype(BF16)
            ga_own = jnp.where(own, ga_wide, 0.0).astype(BF16)
            scores = jnp.where(same, mm(k, q_own, ((1,), (1,))), NEG_BIG)
            exponent = jnp.exp(scores - jnp.max(scores, axis=0, keepdims=True))
            chance = exponent * (1.0 / jnp.sum(exponent, axis=0, keepdims=True))
            gvs.append(mm(chance.astype(BF16), ga))
            g_chance = mm(v, ga_own, ((1,), (1,)))
            inner = jnp.sum(g_chance * chance, axis=0, keepdims=True)
            g_scores = (chance * (g_chance - inner)).astype(BF16)
            gks.append(mm(g_scores, q_low))
            gqs.append(mm(g_scores, k, ((0,), (0,))))
        gq = jnp.where(first, gqs[0], gqs[1]) * SCALE
        gk = jnp.where(first, gks[0], gks[1])
        g_ref[:, q_at] = (gq * cosine + turned(gq * sine)).astype(BF16)
        g_ref[:, k_at] = (gk * cosine + turned(gk * sine)).astype(BF16)
        g_ref[:, v_at] = jnp.where(first, gvs[0], gvs[1]).astype(BF16)


def attention_specs(block):
    table = pl.BlockSpec((block, LANES), lambda b, h, *_: (b, 0))
    column = pl.BlockSpec((1, block, 1), lambda b, h, *_: (b, 0, 0))
    row = pl.BlockSpec((1, 1, block), lambda b, h, *_: (b, 0, 0))
    return [table, table, column, row]


def attention_forward(normed, weights, cosine, sine, seg_ids):
    blocks, block = seg_ids.shape
    rows, width = normed.shape
    part = 3 * width // PARTS
    table, _, column, row = attention_specs(block)

    def turn_around(spec):
        return pl.BlockSpec(spec.block_shape, lambda h, b: spec.index_map(b, h))

    return pl.pallas_call(
        forward_kernel,
        grid=(PARTS, blocks),
        in_specs=[
            pl.BlockSpec((block, width), lambda h, b: (b, 0)),
            pl.BlockSpec((width, part), lambda h, b: (0, h)),
        ]
        + [turn_around(spec) for spec in (table, table, column, row)],
        out_specs=[
            pl.BlockSpec((block, part), lambda h, b: (b, h)),
            pl.BlockSpec((block, part // 3), lambda h, b: (b, h)),
        ],
        out_shape=[
            jax.ShapeDtypeStruct((rows, 3 * width), BF16),
            jax.ShapeDtypeStruct((rows, width), BF16),
        ],
        scratch_shapes=[pltpu.VMEM((block, part), F32)],
        name="attention_forward",
    )(normed, weights, cosine, sine, seg_ids[:, :, None], seg_ids[:, None, :])


def attention_backward(qkv, grad_att, cosine, sine, seg_ids, start, parts):
    blocks, block = seg_ids.shape
    wide, narrow = qkv.shape[1] // PARTS, grad_att.shape[1] // PARTS

    def kernel(start_ref, *refs):
        backward_kernel(*refs)

    return pl.pallas_call(
        kernel,
        grid_spec=pltpu.PrefetchScalarGridSpec(
            num_scalar_prefetch=1,
            grid=(blocks, parts),
            in_specs=[
                pl.BlockSpec((block, wide), lambda b, h, start_ref: (b, start_ref[0] + h)),
                pl.BlockSpec((block, narrow), lambda b, h, start_ref: (b, start_ref[0] + h)),
            ]
            + attention_specs(block),
            out_specs=pl.BlockSpec((block, wide), lambda b, h, start_ref: (b, h)),
        ),
        out_shape=jax.ShapeDtypeStruct((qkv.shape[0], wide * parts), BF16),
        name="attention_backward",
    )(start[None], qkv, grad_att, cosine, sine, seg_ids[:, :, None], seg_ids[:, None, :])


def tables(seg_ids):
    column = lax.broadcasted_iota(jnp.int32, seg_ids.shape, 1)
    before = jnp.concatenate([jnp.full_like(seg_ids[:, :1], -1), seg_ids[:, :-1]], axis=1)
    starts = lax.cummax(jnp.where(seg_ids != before, column, 0), axis=1)
    offsets = (column - starts).reshape(-1)
    halves = HEAD_DIM // 2
    frequency = jnp.power(F32(THETA), -(jnp.arange(halves, dtype=F32) * 2.0 / HEAD_DIM))
    angles = offsets.astype(F32)[:, None] * frequency[None, :]
    cosine, sine = jnp.cos(angles), jnp.sin(angles)
    return (
        jnp.concatenate([cosine] * 4, axis=1),
        jnp.concatenate([-sine, sine, -sine, sine], axis=1),
    )


def mlp_backward_kernel(gain_ref, inv_ref, gate_ref, up_ref, wg_ref, wu_ref, unit_ref, dy_ref, g_ref, low_ref, sums):
    step = pl.program_id(0)
    block = wg_ref.shape[0]
    part = mm(gate_ref[...], wg_ref[...], ((1,), (1,))) + mm(up_ref[...], wu_ref[...], ((1,), (1,)))
    sums[:, pl.ds(pl.multiple_of(step * block, block), block)] = part

    @pl.when(step == pl.num_programs(0) - 1)
    def _():
        rows = sums.shape[0] // 8

        def some(i, carry):
            at = pl.ds(pl.multiple_of(i * rows, rows), rows)
            inner = norm_backward(sums[at, :], unit_ref[at, :], inv_ref[at, :], gain_ref[...])
            total = dy_ref[at, :].astype(F32) + inner
            g_ref[at, :] = total
            low_ref[at, :] = total.astype(BF16)
            return carry

        lax.fori_loop(0, 8, some, 0)


def mlp_backward(gain, inv_scale, grad_gate, grad_up, weights, unit_rows, cotangent):
    tokens, padded = grad_gate.shape
    width = unit_rows.shape[1]
    block = 256

    def whole(array):
        return pl.BlockSpec(array.shape, lambda i: (0, 0), pipeline_mode=pl.Buffered(1))

    result = pl.BlockSpec((tokens, width), lambda i: (0, 0))
    return pl.pallas_call(
        mlp_backward_kernel,
        grid=(width // block,),
        in_specs=[
            whole(gain),
            whole(inv_scale),
            whole(grad_gate),
            whole(grad_up),
            pl.BlockSpec((block, padded), lambda i: (i, 0)),
            pl.BlockSpec((block, padded), lambda i: (i, 1)),
            whole(unit_rows),
            whole(cotangent),
        ],
        out_specs=[result, result],
        out_shape=[
            jax.ShapeDtypeStruct((tokens, width), F32),
            jax.ShapeDtypeStruct((tokens, width), BF16),
        ],
        scratch_shapes=[pltpu.VMEM((tokens, width), F32)],
        compiler_params=pltpu.CompilerParams(vmem_limit_bytes=56 * 2**20),
        name="mlp_backward",
    )(gain, inv_scale, grad_gate, grad_up, weights, weights, unit_rows, cotangent)


def gelu_exact(field):
    return 0.5 * field * (1.0 + lax.erf(field * ROOT_HALF))


def gelu_slope(field):
    return (
        0.5 * (1.0 + lax.erf(field * ROOT_HALF))
        + field * jnp.exp(-0.5 * field * field) * INV_ROOT_TWO_PI
    )


def norm_unit(field):
    center = field - jnp.mean(field, axis=-1, keepdims=True)
    inv_scale = lax.rsqrt(jnp.mean(center * center, axis=-1, keepdims=True) + EPSILON)
    return center * inv_scale, inv_scale


def norm_backward(gradient, unit_rows, inv_scale, gain_row):
    scaled = gradient * gain_row
    inner = (
        scaled
        - jnp.mean(scaled, axis=-1, keepdims=True)
        - unit_rows * jnp.mean(scaled * unit_rows, axis=-1, keepdims=True)
    )
    return inv_scale * inner


def shards(tokens, seg_ids, w_qkv, w_attn_out, w_in, w_down, gain_attn, gain_mlp, cotangent):
    model_width = tokens.shape[1]
    hidden_units = w_down.shape[0]
    padded = up_to(hidden_units, LANES)
    extra = ((0, 0), (0, padded - hidden_units))

    def by_part(field):
        parts = field.reshape(field.shape[0], 3, PARTS, -1)
        return parts.swapaxes(1, 2).reshape(field.shape)

    gains = jnp.pad(jnp.stack([gain_attn, gain_mlp], axis=1), ((0, 0), (0, LANES - 2)))
    rest = lax.all_gather(
        jnp.concatenate(
            [
                jnp.pad(w_in[:, :hidden_units], extra),
                jnp.pad(w_in[:, hidden_units:], extra),
                jnp.pad(w_down.T, extra),
                w_attn_out,
            ],
            axis=1,
        ),
        "dp",
        axis=0,
        tiled=True,
    )
    inputs = tokens.astype(F32)
    first, (cosine, sine, unit_attn, inv_attn) = gather_rows(
        jnp.concatenate([by_part(w_qkv), gains], axis=1), tables(seg_ids) + norm_unit(inputs)
    )
    core = (lax.axis_index("dp") & 1).astype(jnp.int32)
    other = 1 - core
    own_order, other_order = sum_order(core, model_width), sum_order(other, model_width)

    def ordered(field):
        return mm(field, own_order).astype(BF16), mm(field, other_order).astype(BF16)

    dy_own, dy_other = ordered(cotangent)
    wq = first[:, : 3 * model_width]
    gain_rows = first[:, 3 * model_width :].astype(F32).T
    ga, gm = gain_rows[0:1], gain_rows[1:2]

    normed_attn = (unit_attn * ga).astype(BF16)
    attn_own, attn_other = ordered(normed_attn)
    qkv, attended = attention_forward(normed_attn, first, cosine, sine, seg_ids)
    att_own, att_other = ordered(attended)
    rest, att_own, att_other, attn_own, attn_other, dy_own, dy_other = lax.optimization_barrier(
        (rest, att_own, att_other, attn_own, attn_other, dy_own, dy_other)
    )
    wg, wu, wd = (rest[:, i * padded : (i + 1) * padded] for i in range(3))
    wo = rest[:, 3 * padded :]
    resid = inputs + mm(attended, wo)
    unit_mlp, inv_mlp = norm_unit(resid)
    normed_mlp = (unit_mlp * gm).astype(BF16)
    mlp_own, mlp_other, normed_mlp = lax.optimization_barrier(ordered(normed_mlp) + (normed_mlp,))
    gate = mm(normed_mlp, wg)
    upward = mm(normed_mlp, wu)
    activated = gelu_exact(gate)
    hidden = (activated * upward).astype(BF16)

    grad_out = cotangent.astype(F32)
    clock = Clock()
    turn = ((0,), (0,))

    def columns(field, start, width):
        return lax.dynamic_slice_in_dim(field, start, width, 1)

    def weight_gradient(rows, cols):
        return mm(rows, cols, turn).astype(BF16)

    def reduction(rows, cols, came):
        half = rows.shape[1] // 2
        given = mm(rows[:, :half], cols, turn) + came[:half].astype(F32)
        held = mm(rows[:, half:], cols, turn) + came[half:].astype(F32)
        return Reduction(given.astype(BF16), held)

    half_down = up_to(padded // 2, LANES)
    shift = padded - half_down
    down_send = Send(weight_gradient(dy_other, columns(hidden, other * shift, half_down)))
    clock.end(down_send.value)

    (dy,) = clock.stage((cotangent,), [down_send])
    grad_hidden = mm(dy, wd)
    grad_gate = (grad_hidden * upward * gelu_slope(gate)).astype(BF16)
    grad_up = (grad_hidden * activated).astype(BF16)
    grad_own = jnp.where(core == 0, grad_gate, grad_up)
    grad_other = jnp.where(core == 0, grad_up, grad_gate)
    clock.end(grad_own, grad_other)

    (rhs,) = clock.stage((grad_other,))
    in_send = Send(weight_gradient(mlp_other, rhs))
    clock.end(in_send.value)

    (rhs,) = clock.stage(
        (columns(hidden, core * shift, half_down),), [in_send, down_send.landed()]
    )
    down_sum = reduction(dy_own, rhs, down_send.arrived)
    clock.end(down_sum.held)

    (rhs,) = clock.stage((grad_own,), [down_sum, in_send.landed()])
    in_sum = reduction(mlp_own, rhs, in_send.arrived)
    clock.end(in_sum.held)

    lhs, rhs = clock.stage((grad_gate, grad_up), [in_sum])
    grad_resid, grad_resid_b = mlp_backward(gm, inv_mlp, lhs, rhs, rest, unit_mlp, cotangent)
    clock.end(grad_resid_b)

    (grad_resid_b,) = clock.stage((grad_resid_b,), [down_sum])
    half_out = model_width // 2
    out_send = Send(weight_gradient(att_other, columns(grad_resid_b, other * half_out, half_out)))
    clock.end(out_send.value)

    (lhs,) = clock.stage((grad_resid_b,), [out_send])
    grad_att = mm(lhs, wo, ((1,), (1,))).astype(BF16)
    clock.end(grad_att)

    def heads(grad, part, parts):
        return attention_backward(qkv, grad, cosine, sine, seg_ids, part, parts)

    (grad,) = clock.stage((grad_att,), [out_send.landed()])
    g_other = heads(grad, 2 * other, 2)
    clock.end(g_other)

    (rhs,) = clock.stage((g_other,), [down_sum, in_sum])
    qkv_send = Send(weight_gradient(attn_other, rhs))
    clock.end(qkv_send.value)

    (grad,) = clock.stage((grad_att,), [qkv_send])
    g_first = heads(grad, 2 * core, 1)
    clock.end(g_first)

    (rhs,) = clock.stage((g_first,), [down_sum, in_sum, qkv_send.landed()])
    half = 3 * model_width // 2
    quarter = half // 2
    out_sum = reduction(att_own, columns(grad_resid_b, core * half_out, half_out), out_send.arrived)
    q0_sum = reduction(attn_own, rhs, qkv_send.arrived[:, :quarter]).beside(out_sum)
    clock.end(q0_sum.held)

    (grad,) = clock.stage((grad_att,), [q0_sum])
    g_second = heads(grad, 2 * core + 1, 1)
    clock.end(g_second)

    (rhs,) = clock.stage((g_second,), [in_sum])
    q1_sum = reduction(attn_own, rhs, qkv_send.arrived[:, quarter:])
    clock.end(q1_sum.held)

    lhs, g_first, g_second = clock.stage((g_other, g_first, g_second), [q1_sum, q0_sum])
    grads = jnp.zeros((lhs.shape[0], 2 * half), BF16)
    grads = lax.dynamic_update_slice(grads, lhs, (0, other * half))
    grads = lax.dynamic_update_slice(grads, g_first, (0, core * half))
    grads = lax.dynamic_update_slice(grads, g_second, (0, core * half + quarter))
    grad_normed_attn = mm(grads, wq, ((1,), (1,)))
    clock.end(grad_normed_attn)

    (grad_normed_attn,) = clock.stage((grad_normed_attn,), [q1_sum, q0_sum])
    tokens_grad = grad_resid + norm_backward(grad_normed_attn, unit_attn, inv_attn, ga)
    clock.end(tokens_grad)

    (lhs,) = clock.stage((hidden,), [q1_sum, q0_sum])
    out = (resid + mm(lhs, wd, ((1,), (1,)))).astype(BF16)
    clock.end(out)
    reductions = [q1_sum, q0_sum, down_sum, in_sum]
    while not all(r.done() for r in reductions):
        clock.stage((), reductions)
        clock.end()
    for reduction in (down_sum, in_sum):
        reduction.arrived, _ = lax.optimization_barrier((reduction.arrived, out))

    def both_halves(*totals):
        total = jnp.concatenate(totals, axis=1)
        rows = total.shape[0] // 2
        mine = lax.dynamic_slice_in_dim(total, core * rows, rows, 0)
        came = to_partner(lax.dynamic_slice_in_dim(total, other * rows, rows, 0))
        low = jnp.where(core == 0, mine, came)
        high = jnp.where(core == 0, came, mine)
        cuts = [sum(t.shape[1] for t in totals[: i + 1]) for i in range(len(totals) - 1)]
        return zip(jnp.split(low, cuts, axis=1), jnp.split(high, cuts, axis=1))

    first_sum = q0_sum.result()
    (
        (down_low, down_high),
        (gate_rows, up_rows),
        (first_low, first_high),
        (out_low, out_high),
        (last_low, last_high),
    ) = both_halves(
        down_sum.result(),
        in_sum.result(),
        first_sum[:, :quarter],
        first_sum[:, quarter:],
        q1_sum.result(),
    )
    grad_wo = jnp.concatenate([out_low, out_high], axis=1)
    quarters = [first_low, last_low, first_high, last_high]
    size = model_width // PARTS
    grad_qkv = jnp.concatenate(
        [q[:, which * size : (which + 1) * size] for which in range(3) for q in quarters], axis=1
    )
    grad_down = jnp.concatenate([down_low[:, :shift], down_high], axis=1)
    grad_in = jnp.concatenate([gate_rows[:, :hidden_units], up_rows[:, :hidden_units]], axis=1)

    def gain_gradient(weight, gradient, gain):
        return jnp.sum(weight.astype(F32) * gradient, axis=1) / gain.astype(F32)

    return (
        out,
        tokens_grad,
        grad_qkv,
        grad_wo,
        grad_in,
        grad_down[:, :hidden_units].T,
        gain_gradient(w_qkv, grad_qkv, gain_attn),
        gain_gradient(w_in, grad_in, gain_mlp),
    )


def solution(mesh):
    rows = P("dp", None)
    return jax.shard_map(
        shards,
        mesh=mesh,
        in_specs=(rows, rows, rows, rows, rows, P(None, "dp"), P("dp"), P("dp"), rows),
        out_specs=(rows, rows, rows, rows, rows, P(None, "dp"), P("dp"), P("dp")),
        check_vma=False,
    )
```
